32 devices in a mesh: grp: 4 (over y, x), col: 8 (over z, core).
Axes of the slice: x: 2, y: 2, z: 4, core: 2. Of those that a mesh axis runs over, the one named last changes fastest.
Arguments:
- right_side: float32 [2048, 2048], P('grp', 'col'), may hold values from -6 to 6
- solved_factor: float32 [2048, 6144], P('grp', 'col'), may hold values from -0.078125 to 0.078125
- solved_users: float32 [6144, 2048], P('col'), may hold values from -6 to 6
- diag_inverse: float32 [2048, 512], P('grp'), may hold values from -0.25 to 0.25
- coupling: float32 [2048, 1536], P('grp'), may hold values from -0.25 to 0.25
Outputs:
- solution: float32 [2048, 2048], P('grp', 'col')
The draws below stay inside these ranges and needn't reach their ends.
All inputs are finite; a program needn't handle non-finite values.
Results may differ from the reference program's by a relative error of at most 0.0001.
Values sent between devices are 32-bit elements; how exact they have to be, the bound alone decides.
A program may use at most 64 MiB of HBM per device.

```python
import jax
import jax.numpy as jnp
from jax import lax

ITEMS = 2048
BLOCK = 512
SOLVED = 6144
WINDOW = 2048
N_GRP = 4


def with_spikes(entries, rng, source, target, parts, factor):
    owner, partner = [(jnp.arange(entries.shape[axis_at]) // (entries.shape[axis_at] // parts)).reshape([-1 if axis == axis_at else 1 for axis in range(entries.ndim)]) for axis_at in (source, target)]
    chosen = jax.random.permutation(rng, parts)[partner]
    strong = (owner == chosen) | (owner == (partner + parts // 2) % parts)
    return jnp.where(strong, factor * entries, entries)


def levels(own_key, dims, cuts, low, high):
    level = 1.0
    for axis_at, parts in cuts:
        heights = jax.random.uniform(jax.random.fold_in(jax.random.fold_in(own_key, 6), axis_at), (parts,), jnp.float32, low / len(cuts), high / len(cuts))
        level = level * jnp.repeat(jnp.exp(heights), dims[axis_at] // parts).reshape((-1,) + (1,) * (len(dims) - 1 - axis_at))
    return level


def normal_values(rng, shape, width, reach, split=(), kind=jnp.bfloat16):
    values = jax.random.normal(rng, shape, jnp.float32) * width
    if len(split) > 0:
        values = levels(rng, shape, split, -0.22, 0.18) * values
    return jnp.clip(values, min=-reach, max=reach).astype(kind)


def noise_with(stream_key, extent, scale, reach, cuts, heavy, kind=jnp.bfloat16):
    entries = scale * jax.random.normal(stream_key, extent, jnp.float32)
    if cuts:
        entries = entries * levels(stream_key, extent, cuts, -0.22, 0.18)
    return jnp.clip(with_spikes(entries, jax.random.fold_in(stream_key, 3), *heavy), -reach, reach).astype(kind)


def setup_inputs(seed: int = 0) -> dict:
    arg_keys = jax.random.split(jax.random.key(seed), 6)
    return {
        "right_side": normal_values(arg_keys[0], (WINDOW, ITEMS), 1.0, 6.0, ((0, 4), (1, 8)), jnp.float32),
        "solved_factor": normal_values(arg_keys[1], (WINDOW, SOLVED), SOLVED ** -0.5, 0.078125, ((0, 4), (1, 8)), jnp.float32),
        "solved_users": noise_with(arg_keys[2], (SOLVED, ITEMS), 1.0, 6.0, ((0, 8),), (0, 1, 8, 2.0), jnp.float32),
        "diag_inverse": normal_values(arg_keys[3], (WINDOW, BLOCK), BLOCK ** -0.5, 0.25, ((0, 4),), jnp.float32),
        "coupling": normal_values(arg_keys[4], (WINDOW, BLOCK * (N_GRP - 1)), BLOCK ** -0.5, 0.25, ((0, 4),), jnp.float32),
    }


highest = lax.Precision.HIGHEST


def product(left, right):
    return jnp.dot(left, right, precision=highest, preferred_element_type=jnp.float32)


def reference(right_side, solved_factor, solved_users, diag_inverse, coupling):
    reduced = right_side - product(solved_factor, solved_users)
    solved_blocks = []
    for group in range(N_GRP):
        rows = slice(group * BLOCK, (group + 1) * BLOCK)
        residue = reduced[rows]
        for earlier in range(group):
            coupling_block = coupling[rows, earlier * BLOCK:(earlier + 1) * BLOCK]
            residue = residue - product(coupling_block, solved_blocks[earlier])
        solved_blocks.append(product(diag_inverse[rows], residue))
    return jnp.concatenate(solved_blocks, axis=0)
```

```python
import functools

import jax
import jax.numpy as jnp
from jax import lax
from jax.experimental import pallas as pl
from jax.experimental.pallas import tpu as pltpu
from jax.sharding import PartitionSpec as P

highest = lax.Precision.HIGHEST
MESH = pl.DeviceIdType.MESH
LANES = 128
PIECE = 32
LAG = 1
WAIT = 2
JOIN = 6


def broadcast(block, axis, source):
    block = jnp.where(lax.axis_index(axis) == source, block, jnp.zeros_like(block))
    return lax.psum(block, axis)


def apply_plain(matrix, vector):
    return jnp.dot(matrix, vector, precision=highest, preferred_element_type=jnp.float32)


def run_chain(residue, diag_inverse, coupling, apply_left):
    groups = lax.axis_size("grp")
    position = lax.axis_index("grp")
    block_rows = diag_inverse.shape[0]
    result = jnp.zeros_like(residue)
    for section_index in range(groups):
        candidate = apply_left(diag_inverse, residue)
        result = jnp.where(position == section_index, candidate, result)
        if section_index + 1 < groups:
            solved = broadcast(candidate, "grp", section_index)
            coupling_block = coupling[
                :, section_index * block_rows : (section_index + 1) * block_rows
            ]
            residue = jnp.where(
                position > section_index, residue - apply_left(coupling_block, solved), residue
            )
    return result


def by_collectives(right_side, solved_factor, solved_users, diag_inverse, coupling):
    partials = jnp.dot(
        solved_factor, solved_users, precision=highest, preferred_element_type=jnp.float32
    )
    shares = lax.psum_scatter(partials, "col", scatter_dimension=1, tiled=True)
    residue = right_side - shares
    return run_chain(residue, diag_inverse, coupling, apply_plain)


def halves(x):
    high = x.astype(jnp.bfloat16)
    return high, (x - high.astype(jnp.float32)).astype(jnp.bfloat16)


def left_form(x):
    high, low = halves(x)
    return jnp.concatenate([high, high, low], axis=1)


def right_form(x):
    high, low = halves(x)
    return jnp.concatenate([high, low, high], axis=0)


def dot(a, b):
    return jnp.dot(a, b, preferred_element_type=jnp.float32)


def apply_right(rows, matrix):
    count = rows.shape[0]
    high, low = halves(rows)
    both = dot(jnp.concatenate([high, low], axis=0), matrix[0])
    return both[:count] + both[count:] + dot(high, matrix[1])


def kernel(
    groups, chips, pieces, pairs,
    rhs_hbm, factor_hbm, users_hbm, diag_hbm, coupling_hbm,
    out_ref,
    rhs, factor, users, diag, coupling,
    factor3, diag3, rhs_t, diag_t, mix_t, mix, mix_in,
    own, give, take, from_low, from_high, ready, got, result,
    load_sem, users_sem, give_sem, take_sem, hop_sem, low_sem, high_sem,
    ready_sem, got_sem, mix_send_sem, mix_sem, pass_sem, passed_sem,
):
    g = lax.axis_index("grp")
    c = lax.axis_index("col")
    z = c // 2
    e = c % 2
    rows, width = rhs.shape
    half = rows // 2
    size = width // pieces
    last = chips - 1
    partner = (g, z * 2 + (1 - e))
    lower = 2 * z < chips

    barrier = pltpu.get_barrier_semaphore()
    pl.semaphore_signal(barrier, inc=1, device_id=partner, device_id_type=MESH)
    for step in range(1, groups):
        pl.semaphore_signal(
            barrier, inc=1, device_id=((g + step) % groups, c), device_id_type=MESH)

    @pl.when(z > 0)
    def _():
        pl.semaphore_signal(barrier, inc=1, device_id=(g, c - 2), device_id_type=MESH)

    @pl.when(z < last)
    def _():
        pl.semaphore_signal(barrier, inc=1, device_id=(g, c + 2), device_id_type=MESH)

    def chip_at(j):
        if j == last:
            return z
        high, low = last - j, j
        return jnp.where(
            lower, jnp.where(high <= z, high - 1, high), jnp.where(low >= z, low + 1, low))

    factor_load = pltpu.make_async_copy(factor_hbm, factor, load_sem.at[0])
    later = [
        pltpu.make_async_copy(diag_hbm, diag, load_sem.at[1]),
        pltpu.make_async_copy(coupling_hbm, coupling, load_sem.at[2]),
        pltpu.make_async_copy(rhs_hbm, rhs, load_sem.at[3]),
    ]

    def users_load(j, part):
        side = e if part else 1 - e
        column = pl.multiple_of((chip_at(j) * 2 + side) * width, width)
        return pltpu.make_async_copy(
            users_hbm.at[:, pl.ds(column, width)], users.at[2 * j + part],
            users_sem.at[2 * j + part])

    factor_load.start()
    for j in range(chips):
        for part in range(2):
            users_load(j, part).start()
    for copy in later:
        copy.start()

    def span(p):
        return pl.ds(pl.multiple_of(p * size, size), size)

    def give_copy(d, p):
        return pltpu.make_async_remote_copy(
            src_ref=give.at[d, span(p)], dst_ref=take.at[d, span(p)],
            send_sem=give_sem.at[d, p], recv_sem=take_sem.at[d, p],
            device_id=partner, device_id_type=MESH)

    def up(d, p):
        return pltpu.make_async_remote_copy(
            src_ref=own.at[d, span(p)], dst_ref=from_low.at[d, span(p)],
            send_sem=hop_sem.at[d, p], recv_sem=low_sem.at[d, p],
            device_id=(g, c + 2), device_id_type=MESH)

    def down(d, p):
        return pltpu.make_async_remote_copy(
            src_ref=own.at[d, span(p)], dst_ref=from_high.at[d, span(p)],
            send_sem=hop_sem.at[d, p], recv_sem=high_sem.at[d, p],
            device_id=(g, c - 2), device_id_type=MESH)

    def product(j, part):
        users_load(j, part).wait()
        block = dot(factor3[...], right_form(users[2 * j + part])).T
        (own if part else give)[chip_at(j)] = block

    def pair_up(d, at_once):
        @pl.loop(0, pieces)
        def _(p):
            give_copy(d, p).wait()
            own[d, span(p)] = own[d, span(p)] + take[d, span(p)]
            for r, i in at_once:
                @pl.when(p == i)
                def _():
                    launch(r, i)

    def launch(r, p):
        @pl.when(z == 0)
        def _():
            up(last - r, p).start()

        @pl.when(z == last)
        def _():
            down(r, p).start()

    def give_all(d):
        @pl.loop(0, pieces)
        def _(p):
            give_copy(d, p).start()

    def relay_up(r, p):
        d = last - r

        @pl.when(jnp.logical_and(z > 0, d > z))
        def _():
            up(d, p).wait_recv()
            own[d, span(p)] = own[d, span(p)] + from_low[d, span(p)]
            up(d, p).start()

    def relay_down(d, p):
        @pl.when(jnp.logical_and(z < last, d < z))
        def _():
            down(d, p).wait_recv()
            own[d, span(p)] = own[d, span(p)] + from_high[d, span(p)]
            down(d, p).start()

    def relay_near(q):
        for r in range(chips - 2):
            p = q - leads[r]

            @pl.when(jnp.logical_and(p >= 0, p < pieces))
            def _():
                @pl.when(lower)
                def _():
                    relay_up(r, p)

                @pl.when(jnp.logical_not(lower))
                def _():
                    relay_down(r, p)

    def relay_far(q):
        for r in range(chips // 2 - 1):
            p = q - leads[r]

            @pl.when(jnp.logical_and(p >= 0, p < pieces))
            def _():
                @pl.when(lower)
                def _():
                    relay_down(r, p)

                @pl.when(jnp.logical_not(lower))
                def _():
                    relay_up(r, p)

    def mix_copy(k, h, target):
        part = pl.ds(pl.multiple_of(e * half, half), half)
        i = pairs.index((k, h))
        return pltpu.make_async_remote_copy(
            src_ref=mix.at[h, part], dst_ref=mix_in.at[i, part],
            send_sem=mix_send_sem.at[i, target], recv_sem=mix_sem.at[i],
            device_id=(target, c), device_id_type=MESH)

    def mix_pass(k, h):
        part = pl.ds(pl.multiple_of(e * half, half), half)
        i = pairs.index((k, h))
        return pltpu.make_async_remote_copy(
            src_ref=mix_in.at[i, part], dst_ref=mix_in.at[i, part],
            send_sem=pass_sem.at[i], recv_sem=passed_sem.at[i],
            device_id=partner, device_id_type=MESH)

    def prepare():
        for copy in later:
            copy.wait()
        diag3[...] = left_form(diag[...])
        for h in range(groups - 1):
            @pl.when(h < g)
            def _():
                mix[h] = dot(diag3[...], right_form(coupling[:, h * rows : (h + 1) * rows]))
        for k, h in pairs:
            for target in range(k + 1, groups):
                @pl.when(g == k)
                def _():
                    mix_copy(k, h, target).start()

    def turn():
        rhs_t[...] = rhs[...].T
        high, low = halves(diag[...].T)
        diag_t[0] = high
        diag_t[1] = low

    def pass_mix():
        for k, h in pairs:
            @pl.when(g > k)
            def _():
                mix_copy(k, h, k + 1).wait_recv()
                mix_pass(k, h).start()

    def join_mix():
        for k, h in reversed(pairs):
            @pl.when(g > k)
            def _():
                mix_pass(k, h).wait()
                mix[h] = mix[h] - dot(left_form(mix[k]), right_form(mix_in[pairs.index((k, h))]))
        for h in range(groups - 1):
            @pl.when(h < g)
            def _():
                high, low = halves(mix[h].T)
                mix_t[h, 0] = high
                mix_t[h, 1] = low

    def ready_copy(source, buffer, target, p):
        return pltpu.make_async_remote_copy(
            src_ref=buffer.at[span(p)], dst_ref=got.at[source, span(p)],
            send_sem=ready_sem.at[target, p], recv_sem=got_sem.at[source, p],
            device_id=(target, c), device_id_type=MESH)

    def finish(p):
        @pl.when(z > 0)
        def _():
            up(z, p).wait_recv()
            own[z, span(p)] = own[z, span(p)] + from_low[z, span(p)]

        @pl.when(z < last)
        def _():
            down(z, p).wait_recv()
            own[z, span(p)] = own[z, span(p)] + from_high[z, span(p)]

        ready[span(p)] = apply_right(rhs_t[span(p)] - own[z, span(p)], diag_t)

        @pl.when(g < groups - 2)
        def _():
            for target in range(groups - 1, 0, -1):
                @pl.when(target > g)
                def _():
                    ready_copy(g, ready, target, p).start()

    def solve(p):
        result[span(p)] = ready[span(p)]
        for h in range(groups - 1):
            @pl.when(h < g)
            def _():
                ready_copy(h, ready, 0, p).wait_recv()
                result[span(p)] = result[span(p)] - apply_right(got[h, span(p)], mix_t.at[h])

        @pl.when(g == groups - 2)
        def _():
            ready_copy(g, result, groups - 1, p).start()

        per = LANES // size

        @pl.when(p % per == per - 1)
        def _():
            columns = pl.ds(pl.multiple_of((p // per) * LANES, LANES), LANES)
            out_ref[:, columns] = result[columns, :].T

    leads = [r + 1 if r else 0 for r in range(chips - 1)]
    order = [
        (r, q - leads[r]) for q in range(pieces + leads[-1]) for r in range(chips - 1)
        if 0 <= q - leads[r] < pieces]
    factor_load.wait()
    factor3[...] = left_form(factor[...])
    product(0, 0)
    product(0, 1)
    pl.semaphore_wait(
        barrier, groups + jnp.where(z > 0, 1, 0) + jnp.where(z < last, 1, 0))
    give_all(chip_at(0))
    for j in range(chips):
        if j + 1 < chips:
            product(j + 1, 0)
            give_all(chip_at(j + 1))
        open_now = []
        while order and order[0][0] <= j:
            open_now.append(order.pop(0))
        pair_up(chip_at(j), open_now if j == 0 else [])
        for r, p in open_now if j else []:
            launch(r, p)
        if j + 1 < chips:
            product(j + 1, 1)
        if j == chips - 2:
            prepare()

    turn()
    edge = jnp.logical_or(z == 0, z == last)
    behind = jnp.where(edge, chips // 2, leads[-1])
    extra = jnp.where(g == groups - 1, 2 * WAIT, WAIT)

    @pl.loop(0, pieces + leads[-1] + 2 * WAIT)
    def _(q):
        relay_near(q)
        p = q - behind

        @pl.when(jnp.logical_and(p >= 0, p < pieces))
        def _():
            finish(p)

        relay_far(q - LAG)

        @pl.when(q == JOIN - 1)
        def _():
            pass_mix()

        @pl.when(q == JOIN)
        def _():
            join_mix()

        p = q - behind - extra
        high = jnp.minimum(p + 1, pieces)
        low = jnp.where(q == JOIN, 0, jnp.maximum(p, 0))

        @pl.when(q >= JOIN)
        def _():
            @pl.loop(low, high)
            def _(i):
                solve(i)

    @pl.loop(0, chips)
    def _(d):
        @pl.when(d != z)
        def _():
            for p in range(pieces):
                pltpu.make_async_remote_copy(
                    src_ref=own.at[d, span(p)], dst_ref=from_low.at[d, span(p)],
                    send_sem=hop_sem.at[d, p], recv_sem=low_sem.at[d, p],
                    device_id=partner, device_id_type=MESH).wait_send()

    for target in range(1, groups):
        @pl.when(jnp.logical_and(target > g, jnp.logical_or(g < groups - 2, target == groups - 1)))
        def _():
            for p in range(pieces):
                ready_copy(g, ready, target, p).wait_send()
    for k, h in pairs:
        for target in range(k + 1, groups):
            @pl.when(g == k)
            def _():
                mix_copy(k, h, target).wait_send()


def by_kernel(right_side, solved_factor, solved_users, diag_inverse, coupling):
    groups = lax.axis_size("grp")
    chips = lax.axis_size("col") // 2
    rows, width = right_side.shape
    depth = solved_factor.shape[1]
    pieces = width // PIECE
    pairs = [(k, h) for k in range(1, groups - 2) for h in range(k)]
    f32, bf16 = jnp.float32, jnp.bfloat16
    dma = pltpu.SemaphoreType.DMA
    lines = pltpu.VMEM((chips, width, rows), f32)
    square = (rows, rows)
    scratch = [
        pltpu.VMEM((rows, width), f32),
        pltpu.VMEM((rows, depth), f32),
        pltpu.VMEM((2 * chips, depth, width), f32),
        pltpu.VMEM(square, f32),
        pltpu.VMEM(coupling.shape, f32),
        pltpu.VMEM((rows, 3 * depth), bf16),
        pltpu.VMEM((rows, 3 * rows), bf16),
        pltpu.VMEM((width, rows), f32),
        pltpu.VMEM((2,) + square, bf16),
        pltpu.VMEM((groups - 1, 2) + square, bf16),
        pltpu.VMEM((groups - 1,) + square, f32),
        pltpu.VMEM((max(len(pairs), 1),) + square, f32),
        lines, lines, lines, lines, lines,
        pltpu.VMEM((width, rows), f32),
        pltpu.VMEM((groups - 1, width, rows), f32),
        pltpu.VMEM((width, rows), f32),
        dma((4,)), dma((2 * chips,)), dma((chips, pieces)), dma((chips, pieces)),
        dma((chips, pieces)), dma((chips, pieces)), dma((chips, pieces)),
        dma((groups, pieces)), dma((groups, pieces)),
        dma((max(len(pairs), 1), groups)), dma((max(len(pairs), 1),)),
        dma((max(len(pairs), 1),)), dma((max(len(pairs), 1),)),
    ]
    return pl.pallas_call(
        functools.partial(kernel, groups, chips, pieces, pairs),
        out_shape=pltpu.VMEM((rows, width), f32),
        in_specs=[pl.BlockSpec(memory_space=pl.ANY)] * 5,
        out_specs=pl.BlockSpec(memory_space=pltpu.VMEM),
        scratch_shapes=scratch,
        compiler_params=pltpu.CompilerParams(
            collective_id=0, has_side_effects=True, vmem_limit_bytes=63 << 20),
    )(right_side, solved_factor, solved_users, diag_inverse, coupling)


def on_device(right_side, *others):
    whole_tiles = (
        right_side.shape[1] % LANES == 0 and right_side.shape[0] % LANES == 0
        and lax.axis_size("col") % 2 == 0 and lax.axis_size("col") > 4
        and lax.axis_size("grp") > 1)
    return (by_kernel if whole_tiles else by_collectives)(right_side, *others)


def solution(mesh):
    placed = (P("grp", "col"), P("grp", "col"), P("col", None), P("grp", None), P("grp", None))
    return jax.shard_map(
        on_device, mesh=mesh, in_specs=placed, out_specs=P("grp", "col"), check_vma=False
    )
```

```python
import functools

import jax
import jax.numpy as jnp
from jax import lax
from jax.experimental import pallas as pl
from jax.experimental.pallas import tpu as pltpu
from jax.sharding import PartitionSpec as P

highest = lax.Precision.HIGHEST
MESH = pl.DeviceIdType.MESH
LANES = 128
PIECE = 32
LAG = 1
WAIT = 1
PASS = 5
JOIN = 7
START = 8


def broadcast(block, axis, source):
    block = jnp.where(lax.axis_index(axis) == source, block, jnp.zeros_like(block))
    return lax.psum(block, axis)


def apply_plain(matrix, vector):
    return jnp.dot(matrix, vector, precision=highest, preferred_element_type=jnp.float32)


def run_chain(residue, diag_inverse, coupling, apply_left):
    groups = lax.axis_size("grp")
    position = lax.axis_index("grp")
    block_rows = diag_inverse.shape[0]
    result = jnp.zeros_like(residue)
    for section_index in range(groups):
        candidate = apply_left(diag_inverse, residue)
        result = jnp.where(position == section_index, candidate, result)
        if section_index + 1 < groups:
            solved = broadcast(candidate, "grp", section_index)
            coupling_block = coupling[
                :, section_index * block_rows : (section_index + 1) * block_rows
            ]
            residue = jnp.where(
                position > section_index, residue - apply_left(coupling_block, solved), residue
            )
    return result


def by_collectives(right_side, solved_factor, solved_users, diag_inverse, coupling):
    partials = jnp.dot(
        solved_factor, solved_users, precision=highest, preferred_element_type=jnp.float32
    )
    shares = lax.psum_scatter(partials, "col", scatter_dimension=1, tiled=True)
    residue = right_side - shares
    return run_chain(residue, diag_inverse, coupling, apply_plain)


def halves(x):
    high = x.astype(jnp.bfloat16)
    return high, (x - high.astype(jnp.float32)).astype(jnp.bfloat16)


def left_form(x):
    high, low = halves(x)
    return jnp.concatenate([high, high, low], axis=1)


def right_form(x):
    high, low = halves(x)
    return jnp.concatenate([high, low, high], axis=0)


def dot(a, b):
    return jnp.dot(a, b, preferred_element_type=jnp.float32)


def apply_right(rows, matrix):
    count = rows.shape[0]
    high, low = halves(rows)
    both = dot(jnp.concatenate([high, low], axis=0), matrix[0])
    return both[:count] + both[count:] + dot(high, matrix[1])


def kernel(
    groups, chips, pieces, pairs,
    rhs_hbm, factor_hbm, users_hbm, diag_hbm, coupling_hbm,
    out_ref,
    rhs, factor, users, diag, coupling,
    factor3, diag3, rhs_t, diag_t, mix_t, mix, blend, mix_in,
    own, give, take, from_low, from_high, ready, got, result,
    load_sem, users_sem, give_sem, take_sem, hop_sem, low_sem, high_sem,
    ready_sem, got_sem, mix_send_sem, mix_sem, pass_sem, passed_sem,
):
    g = lax.axis_index("grp")
    c = lax.axis_index("col")
    z = c // 2
    e = c % 2
    rows, width = rhs.shape
    half = rows // 2
    size = width // pieces
    last = chips - 1
    per = LANES // size
    partner = (g, z * 2 + (1 - e))
    lower = 2 * z < chips

    barrier = pltpu.get_barrier_semaphore()
    pl.semaphore_signal(barrier, inc=1, device_id=partner, device_id_type=MESH)
    for step in range(1, groups):
        pl.semaphore_signal(
            barrier, inc=1, device_id=((g + step) % groups, c), device_id_type=MESH)

    @pl.when(z > 0)
    def _():
        pl.semaphore_signal(barrier, inc=1, device_id=(g, c - 2), device_id_type=MESH)

    @pl.when(z < last)
    def _():
        pl.semaphore_signal(barrier, inc=1, device_id=(g, c + 2), device_id_type=MESH)

    def chip_at(j):
        if j == last:
            return z
        high, low = last - j, j
        return jnp.where(
            lower, jnp.where(high <= z, high - 1, high), jnp.where(low >= z, low + 1, low))

    factor_load = pltpu.make_async_copy(factor_hbm, factor, load_sem.at[0])
    later = [
        pltpu.make_async_copy(diag_hbm, diag, load_sem.at[1]),
        pltpu.make_async_copy(coupling_hbm, coupling, load_sem.at[2]),
        pltpu.make_async_copy(rhs_hbm, rhs, load_sem.at[3]),
    ]

    def users_load(j, part):
        side = e if part else 1 - e
        column = pl.multiple_of((chip_at(j) * 2 + side) * width, width)
        return pltpu.make_async_copy(
            users_hbm.at[:, pl.ds(column, width)], users.at[2 * j + part],
            users_sem.at[2 * j + part])

    factor_load.start()
    for j in range(chips):
        for part in range(2):
            users_load(j, part).start()
    for copy in later:
        copy.start()

    def span(p):
        return pl.ds(pl.multiple_of(p * size, size), size)

    def give_copy(d, p):
        return pltpu.make_async_remote_copy(
            src_ref=give.at[d, span(p)], dst_ref=take.at[d, span(p)],
            send_sem=give_sem.at[d, p], recv_sem=take_sem.at[d, p],
            device_id=partner, device_id_type=MESH)

    def up(d, p):
        return pltpu.make_async_remote_copy(
            src_ref=own.at[d, span(p)], dst_ref=from_low.at[d, span(p)],
            send_sem=hop_sem.at[d, p], recv_sem=low_sem.at[d, p],
            device_id=(g, c + 2), device_id_type=MESH)

    def down(d, p):
        return pltpu.make_async_remote_copy(
            src_ref=own.at[d, span(p)], dst_ref=from_high.at[d, span(p)],
            send_sem=hop_sem.at[d, p], recv_sem=high_sem.at[d, p],
            device_id=(g, c - 2), device_id_type=MESH)

    def product(j, part):
        users_load(j, part).wait()
        block = dot(factor3[...], right_form(users[2 * j + part])).T
        (own if part else give)[chip_at(j)] = block

    def pair_up(d, at_once):
        @pl.loop(0, pieces)
        def _(p):
            give_copy(d, p).wait()
            own[d, span(p)] = own[d, span(p)] + take[d, span(p)]
            for r, i in at_once:
                @pl.when(p == i)
                def _():
                    launch(r, i)

    def launch(r, p):
        @pl.when(z == 0)
        def _():
            up(last - r, p).start()

        @pl.when(z == last)
        def _():
            down(r, p).start()

    def give_all(d):
        @pl.loop(0, pieces)
        def _(p):
            give_copy(d, p).start()

    def relay_up(r, p):
        d = last - r

        @pl.when(jnp.logical_and(z > 0, d > z))
        def _():
            up(d, p).wait_recv()
            own[d, span(p)] = own[d, span(p)] + from_low[d, span(p)]
            up(d, p).start()

    def relay_down(d, p):
        @pl.when(jnp.logical_and(z < last, d < z))
        def _():
            down(d, p).wait_recv()
            own[d, span(p)] = own[d, span(p)] + from_high[d, span(p)]
            down(d, p).start()

    def relay_near(q):
        for r in range(chips - 2):
            p = q - leads[r]

            @pl.when(jnp.logical_and(p >= 0, p < pieces))
            def _():
                @pl.when(lower)
                def _():
                    relay_up(r, p)

                @pl.when(jnp.logical_not(lower))
                def _():
                    relay_down(r, p)

    def relay_far(q):
        for r in range(chips // 2 - 1):
            p = q - leads[r]

            @pl.when(jnp.logical_and(p >= 0, p < pieces))
            def _():
                @pl.when(lower)
                def _():
                    relay_down(r, p)

                @pl.when(jnp.logical_not(lower))
                def _():
                    relay_up(r, p)

    def mix_copy(k, h, target):
        part = pl.ds(pl.multiple_of(e * half, half), half)
        i = pairs.index((k, h))
        return pltpu.make_async_remote_copy(
            src_ref=mix.at[h, part], dst_ref=mix_in.at[i, part],
            send_sem=mix_send_sem.at[i, target], recv_sem=mix_sem.at[i],
            device_id=(target, c), device_id_type=MESH)

    def mix_pass(k, h):
        part = pl.ds(pl.multiple_of(e * half, half), half)
        i = pairs.index((k, h))
        return pltpu.make_async_remote_copy(
            src_ref=mix_in.at[i, part], dst_ref=mix_in.at[i, part],
            send_sem=pass_sem.at[i], recv_sem=passed_sem.at[i],
            device_id=partner, device_id_type=MESH)

    def prepare():
        for copy in later:
            copy.wait()
        diag3[...] = left_form(diag[...])
        for h in range(groups - 1):
            @pl.when(h < g)
            def _():
                effect = dot(diag3[...], right_form(coupling[:, h * rows : (h + 1) * rows]))
                mix[h] = effect
                blend[h] = effect
        for k, h in pairs:
            for target in range(k + 1, groups):
                @pl.when(g == k)
                def _():
                    mix_copy(k, h, target).start()

    def turn():
        rhs_t[...] = rhs[...].T
        high, low = halves(diag[...].T)
        diag_t[0] = high
        diag_t[1] = low

    def pass_mix(step):
        for k, h in pairs:
            @pl.when(jnp.logical_and(g > k, step == k - 1))
            def _():
                mix_copy(k, h, k + 1).wait_recv()
                mix_pass(k, h).start()

    def join_mix(step):
        for n, k in enumerate(range(groups - 2, 0, -1)):
            @pl.when(jnp.logical_and(g > k, step == n))
            def _():
                for h in range(k):
                    mix_pass(k, h).wait()
                left = left_form(blend[k])
                for h in range(k):
                    right = right_form(mix_in[pairs.index((k, h))])
                    blend[h] = blend[h] - dot(left, right)

        @pl.when(step == max(groups - 3, 0))
        def _():
            for h in range(groups - 1):
                @pl.when(h < g)
                def _():
                    high, low = halves(blend[h].T)
                    mix_t[h, 0] = high
                    mix_t[h, 1] = low

    def ready_copy(source, target, p):
        return pltpu.make_async_remote_copy(
            src_ref=ready.at[span(p)], dst_ref=got.at[source, span(p)],
            send_sem=ready_sem.at[target, p], recv_sem=got_sem.at[source, p],
            device_id=(target, c), device_id_type=MESH)

    def finish(p):
        @pl.when(z > 0)
        def _():
            up(z, p).wait_recv()
            own[z, span(p)] = own[z, span(p)] + from_low[z, span(p)]

        @pl.when(z < last)
        def _():
            down(z, p).wait_recv()
            own[z, span(p)] = own[z, span(p)] + from_high[z, span(p)]

        ready[span(p)] = apply_right(rhs_t[span(p)] - own[z, span(p)], diag_t)

        for target in range(groups - 1, 0, -1):
            @pl.when(target > g)
            def _():
                ready_copy(g, target, p).start()

    def solve(p, count):
        these = pl.ds(pl.multiple_of(p * size, size), count * size)
        result[these] = ready[these]
        for h in range(groups - 1):
            @pl.when(h < g)
            def _():
                for i in range(count):
                    ready_copy(h, 0, p + i).wait_recv()
                result[these] = result[these] - apply_right(got[h, these], mix_t.at[h])

        @pl.when((p + count) % per == 0)
        def _():
            columns = pl.ds(pl.multiple_of((p // per) * LANES, LANES), LANES)
            out_ref[:, columns] = result[columns, :].T

    leads = [r + 1 if r else 0 for r in range(chips - 1)]
    order = [
        (r, q - leads[r]) for q in range(pieces + leads[-1]) for r in range(chips - 1)
        if 0 <= q - leads[r] < pieces]
    factor_load.wait()
    factor3[...] = left_form(factor[...])
    product(0, 0)
    pl.semaphore_wait(
        barrier, groups + jnp.where(z > 0, 1, 0) + jnp.where(z < last, 1, 0))
    give_all(chip_at(0))
    product(0, 1)
    sender = jnp.logical_and(g > 0, g < groups - 1)
    edge = jnp.logical_or(z == 0, z == last)
    for j in range(chips):
        open_now = []
        while order and order[0][0] <= j:
            open_now.append(order.pop(0))
        if j == 0:
            pair_up(chip_at(0), open_now)
            product(1, 0)
            give_all(chip_at(1))

            @pl.when(jnp.logical_and(sender, jnp.logical_not(edge)))
            def _():
                prepare()

            product(1, 1)
        else:
            if j + 1 < chips:
                product(j + 1, 0)
                give_all(chip_at(j + 1))
            pair_up(chip_at(j), [])
            for r, p in open_now:
                launch(r, p)
            if j == 1:
                @pl.when(jnp.logical_and(sender, edge))
                def _():
                    prepare()

            if j + 1 < chips:
                product(j + 1, 1)

    @pl.when(jnp.logical_not(sender))
    def _():
        prepare()

    turn()
    behind = jnp.where(edge, chips // 2, leads[-1])

    @pl.loop(0, pieces + leads[-1] + WAIT)
    def _(q):
        relay_near(q)
        p = q - behind

        @pl.when(jnp.logical_and(p >= 0, p < pieces))
        def _():
            finish(p)

        relay_far(q - LAG)

        pass_mix(q - PASS)

        join_mix(q - JOIN)
        p = q - behind - WAIT

        @pl.when(q == START)
        def _():
            solve(0, per)

        @pl.when(q >= START)
        def _():
            @pl.loop(jnp.where(q == START, per, jnp.maximum(p, per)), jnp.minimum(p + 1, pieces))
            def _(i):
                solve(i, 1)

    @pl.loop(0, chips)
    def _(d):
        @pl.when(d != z)
        def _():
            for p in range(pieces):
                pltpu.make_async_remote_copy(
                    src_ref=own.at[d, span(p)], dst_ref=from_low.at[d, span(p)],
                    send_sem=hop_sem.at[d, p], recv_sem=low_sem.at[d, p],
                    device_id=partner, device_id_type=MESH).wait_send()

    for target in range(1, groups):
        @pl.when(target > g)
        def _():
            for p in range(pieces):
                ready_copy(g, target, p).wait_send()
    for k, h in pairs:
        for target in range(k + 1, groups):
            @pl.when(g == k)
            def _():
                mix_copy(k, h, target).wait_send()


def by_kernel(right_side, solved_factor, solved_users, diag_inverse, coupling):
    groups = lax.axis_size("grp")
    chips = lax.axis_size("col") // 2
    rows, width = right_side.shape
    depth = solved_factor.shape[1]
    pieces = width // PIECE
    pairs = [(k, h) for k in range(1, groups - 1) for h in range(k)]
    f32, bf16 = jnp.float32, jnp.bfloat16
    dma = pltpu.SemaphoreType.DMA
    lines = pltpu.VMEM((chips, width, rows), f32)
    square = (rows, rows)
    scratch = [
        pltpu.VMEM((rows, width), f32),
        pltpu.VMEM((rows, depth), f32),
        pltpu.VMEM((2 * chips, depth, width), f32),
        pltpu.VMEM(square, f32),
        pltpu.VMEM(coupling.shape, f32),
        pltpu.VMEM((rows, 3 * depth), bf16),
        pltpu.VMEM((rows, 3 * rows), bf16),
        pltpu.VMEM((width, rows), f32),
        pltpu.VMEM((2,) + square, bf16),
        pltpu.VMEM((groups - 1, 2) + square, bf16),
        pltpu.VMEM((groups - 1,) + square, f32),
        pltpu.VMEM((groups - 1,) + square, f32),
        pltpu.VMEM((max(len(pairs), 1),) + square, f32),
        lines, lines, lines, lines, lines,
        pltpu.VMEM((width, rows), f32),
        pltpu.VMEM((groups - 1, width, rows), f32),
        pltpu.VMEM((width, rows), f32),
        dma((4,)), dma((2 * chips,)), dma((chips, pieces)), dma((chips, pieces)),
        dma((chips, pieces)), dma((chips, pieces)), dma((chips, pieces)),
        dma((groups, pieces)), dma((groups, pieces)),
        dma((max(len(pairs), 1), groups)), dma((max(len(pairs), 1),)),
        dma((max(len(pairs), 1),)), dma((max(len(pairs), 1),)),
    ]
    return pl.pallas_call(
        functools.partial(kernel, groups, chips, pieces, pairs),
        out_shape=pltpu.VMEM((rows, width), f32),
        in_specs=[pl.BlockSpec(memory_space=pl.ANY)] * 5,
        out_specs=pl.BlockSpec(memory_space=pltpu.VMEM),
        scratch_shapes=scratch,
        compiler_params=pltpu.CompilerParams(
            collective_id=0, has_side_effects=True, vmem_limit_bytes=63 << 20),
    )(right_side, solved_factor, solved_users, diag_inverse, coupling)


def on_device(right_side, *others):
    whole_tiles = (
        right_side.shape[1] % LANES == 0 and right_side.shape[0] % LANES == 0
        and lax.axis_size("col") % 2 == 0 and lax.axis_size("col") > 4
        and lax.axis_size("grp") > 1)
    return (by_kernel if whole_tiles else by_collectives)(right_side, *others)


def solution(mesh):
    placed = (P("grp", "col"), P("grp", "col"), P("col", None), P("grp", None), P("grp", None))
    return jax.shard_map(
        on_device, mesh=mesh, in_specs=placed, out_specs=P("grp", "col"), check_vma=False
    )
```

```python
import functools

import jax
import jax.numpy as jnp
from jax import lax
from jax.experimental import pallas as pl
from jax.experimental.pallas import tpu as pltpu
from jax.sharding import PartitionSpec as P

highest = lax.Precision.HIGHEST
MESH = pl.DeviceIdType.MESH
LANES = 128
PIECE = 32
LAG = 1
WAIT = 1
PASS = 5
JOIN = 6
START = 7


def broadcast(block, axis, source):
    block = jnp.where(lax.axis_index(axis) == source, block, jnp.zeros_like(block))
    return lax.psum(block, axis)


def apply_plain(matrix, vector):
    return jnp.dot(matrix, vector, precision=highest, preferred_element_type=jnp.float32)


def run_chain(residue, diag_inverse, coupling, apply_left):
    groups = lax.axis_size("grp")
    position = lax.axis_index("grp")
    block_rows = diag_inverse.shape[0]
    result = jnp.zeros_like(residue)
    for section_index in range(groups):
        candidate = apply_left(diag_inverse, residue)
        result = jnp.where(position == section_index, candidate, result)
        if section_index + 1 < groups:
            solved = broadcast(candidate, "grp", section_index)
            coupling_block = coupling[
                :, section_index * block_rows : (section_index + 1) * block_rows
            ]
            residue = jnp.where(
                position > section_index, residue - apply_left(coupling_block, solved), residue
            )
    return result


def by_collectives(right_side, solved_factor, solved_users, diag_inverse, coupling):
    partials = jnp.dot(
        solved_factor, solved_users, precision=highest, preferred_element_type=jnp.float32
    )
    shares = lax.psum_scatter(partials, "col", scatter_dimension=1, tiled=True)
    residue = right_side - shares
    return run_chain(residue, diag_inverse, coupling, apply_plain)


def halves(x):
    high = x.astype(jnp.bfloat16)
    return high, (x - high.astype(jnp.float32)).astype(jnp.bfloat16)


def left_form(x):
    high, low = halves(x)
    return jnp.concatenate([high, high, low], axis=1)


def right_form(x):
    high, low = halves(x)
    return jnp.concatenate([high, low, high], axis=0)


def dot(a, b):
    return jnp.dot(a, b, preferred_element_type=jnp.float32)


def apply_right(rows, matrix):
    count = rows.shape[0]
    high, low = halves(rows)
    both = dot(jnp.concatenate([high, low], axis=0), matrix[0])
    return both[:count] + both[count:] + dot(high, matrix[1])


def kernel(
    groups, chips, pieces, pairs,
    rhs_hbm, factor_hbm, users_hbm, diag_hbm, coupling_hbm,
    out_ref,
    rhs, factor, users, diag, coupling,
    factor3, diag3, rhs_t, diag_t, mix_t, mix, blend, mix_in,
    own, give, take, from_low, from_high, ready, got, result,
    load_sem, users_sem, give_sem, take_sem, hop_sem, low_sem, high_sem,
    ready_sem, got_sem, mix_send_sem, mix_sem, pass_sem, passed_sem,
):
    g = lax.axis_index("grp")
    c = lax.axis_index("col")
    z = c // 2
    e = c % 2
    rows, width = rhs.shape
    half = rows // 2
    size = width // pieces
    last = chips - 1
    per = LANES // size
    partner = (g, z * 2 + (1 - e))
    lower = 2 * z < chips

    barrier = pltpu.get_barrier_semaphore()
    pl.semaphore_signal(barrier, inc=1, device_id=partner, device_id_type=MESH)
    for step in range(1, groups):
        pl.semaphore_signal(
            barrier, inc=1, device_id=((g + step) % groups, c), device_id_type=MESH)

    @pl.when(z > 0)
    def _():
        pl.semaphore_signal(barrier, inc=1, device_id=(g, c - 2), device_id_type=MESH)

    @pl.when(z < last)
    def _():
        pl.semaphore_signal(barrier, inc=1, device_id=(g, c + 2), device_id_type=MESH)

    def chip_at(j):
        if j == last:
            return z
        high, low = last - j, j
        return jnp.where(
            lower, jnp.where(high <= z, high - 1, high), jnp.where(low >= z, low + 1, low))

    factor_load = pltpu.make_async_copy(factor_hbm, factor, load_sem.at[0])
    later = [
        pltpu.make_async_copy(diag_hbm, diag, load_sem.at[1]),
        pltpu.make_async_copy(coupling_hbm, coupling, load_sem.at[2]),
        pltpu.make_async_copy(rhs_hbm, rhs, load_sem.at[3]),
    ]

    def users_load(j, part):
        side = e if part else 1 - e
        column = pl.multiple_of((chip_at(j) * 2 + side) * width, width)
        return pltpu.make_async_copy(
            users_hbm.at[:, pl.ds(column, width)], users.at[2 * j + part],
            users_sem.at[2 * j + part])

    factor_load.start()
    for j in range(chips):
        for part in range(2):
            users_load(j, part).start()
    for copy in later:
        copy.start()

    def span(p):
        return pl.ds(pl.multiple_of(p * size, size), size)

    def give_copy(d, p):
        return pltpu.make_async_remote_copy(
            src_ref=give.at[d, span(p)], dst_ref=take.at[d, span(p)],
            send_sem=give_sem.at[d, p], recv_sem=take_sem.at[d, p],
            device_id=partner, device_id_type=MESH)

    def up(d, p):
        return pltpu.make_async_remote_copy(
            src_ref=own.at[d, span(p)], dst_ref=from_low.at[d, span(p)],
            send_sem=hop_sem.at[d, p], recv_sem=low_sem.at[d, p],
            device_id=(g, c + 2), device_id_type=MESH)

    def down(d, p):
        return pltpu.make_async_remote_copy(
            src_ref=own.at[d, span(p)], dst_ref=from_high.at[d, span(p)],
            send_sem=hop_sem.at[d, p], recv_sem=high_sem.at[d, p],
            device_id=(g, c - 2), device_id_type=MESH)

    def product(j, part):
        users_load(j, part).wait()
        block = dot(factor3[...], right_form(users[2 * j + part])).T
        (own if part else give)[chip_at(j)] = block

    def pair_up(d, at_once):
        @pl.loop(0, pieces)
        def _(p):
            give_copy(d, p).wait()
            own[d, span(p)] = own[d, span(p)] + take[d, span(p)]
            for r, i in at_once:
                @pl.when(p == i)
                def _():
                    launch(r, i)

    def launch(r, p):
        @pl.when(z == 0)
        def _():
            up(last - r, p).start()

        @pl.when(z == last)
        def _():
            down(r, p).start()

    def give_all(d):
        @pl.loop(0, pieces)
        def _(p):
            give_copy(d, p).start()

    def relay_up(r, p):
        d = last - r

        @pl.when(jnp.logical_and(z > 0, d > z))
        def _():
            up(d, p).wait_recv()
            own[d, span(p)] = own[d, span(p)] + from_low[d, span(p)]
            up(d, p).start()

    def relay_down(d, p):
        @pl.when(jnp.logical_and(z < last, d < z))
        def _():
            down(d, p).wait_recv()
            own[d, span(p)] = own[d, span(p)] + from_high[d, span(p)]
            down(d, p).start()

    def relay_near(q):
        for r in range(chips - 2):
            p = q - leads[r]

            @pl.when(jnp.logical_and(p >= 0, p < pieces))
            def _():
                @pl.when(lower)
                def _():
                    relay_up(r, p)

                @pl.when(jnp.logical_not(lower))
                def _():
                    relay_down(r, p)

    def relay_far(q):
        for r in range(chips // 2 - 1):
            p = q - leads[r]

            @pl.when(jnp.logical_and(p >= 0, p < pieces))
            def _():
                @pl.when(lower)
                def _():
                    relay_down(r, p)

                @pl.when(jnp.logical_not(lower))
                def _():
                    relay_up(r, p)

    def mix_copy(k, h, target):
        part = pl.ds(pl.multiple_of(e * half, half), half)
        i = pairs.index((k, h))
        return pltpu.make_async_remote_copy(
            src_ref=mix.at[h, part], dst_ref=mix_in.at[i, part],
            send_sem=mix_send_sem.at[i, target], recv_sem=mix_sem.at[i],
            device_id=(target, c), device_id_type=MESH)

    def mix_pass(k, h):
        part = pl.ds(pl.multiple_of(e * half, half), half)
        i = pairs.index((k, h))
        return pltpu.make_async_remote_copy(
            src_ref=mix_in.at[i, part], dst_ref=mix_in.at[i, part],
            send_sem=pass_sem.at[i], recv_sem=passed_sem.at[i],
            device_id=partner, device_id_type=MESH)

    def couple(h):
        effect = dot(diag3[...], right_form(coupling[:, h * rows : (h + 1) * rows]))
        mix[h] = effect
        blend[h] = effect

        @pl.when(g == h + 1)
        def _():
            high, low = halves(effect.T)
            mix_t[h, 0] = high
            mix_t[h, 1] = low

    def prepare():
        diag3[...] = left_form(diag[...])
        for h in range(groups - 2):
            @pl.when(h < g)
            def _():
                couple(h)
        for k, h in pairs:
            for target in range(k + 1, groups):
                @pl.when(g == k)
                def _():
                    mix_copy(k, h, target).start()

    def turn():
        rhs_t[...] = rhs[...].T
        high, low = halves(diag[...].T)
        diag_t[0] = high
        diag_t[1] = low

    def pass_mix(step):
        for k, h in pairs:
            @pl.when(jnp.logical_and(g > k, step == k - 1))
            def _():
                mix_copy(k, h, k + 1).wait_recv()
                mix_pass(k, h).start()

    def join_mix(step):
        for n, k in enumerate(range(groups - 2, 0, -1)):
            @pl.when(jnp.logical_and(g > k, step == n))
            def _():
                for h in range(k):
                    mix_pass(k, h).wait()
                left = left_form(blend[k])
                for h in range(k):
                    right = right_form(mix_in[pairs.index((k, h))])
                    blend[h] = blend[h] - dot(left, right)

        @pl.when(step == max(groups - 3, 0))
        def _():
            for h in range(groups - 2):
                @pl.when(h < g - 1)
                def _():
                    high, low = halves(blend[h].T)
                    mix_t[h, 0] = high
                    mix_t[h, 1] = low

    def ready_copy(source, target, p):
        return pltpu.make_async_remote_copy(
            src_ref=ready.at[span(p)], dst_ref=got.at[source, span(p)],
            send_sem=ready_sem.at[target, p], recv_sem=got_sem.at[source, p],
            device_id=(target, c), device_id_type=MESH)

    def finish(p):
        @pl.when(z > 0)
        def _():
            up(z, p).wait_recv()
            own[z, span(p)] = own[z, span(p)] + from_low[z, span(p)]

        @pl.when(z < last)
        def _():
            down(z, p).wait_recv()
            own[z, span(p)] = own[z, span(p)] + from_high[z, span(p)]

        ready[span(p)] = apply_right(rhs_t[span(p)] - own[z, span(p)], diag_t)

        for target in range(groups - 1, 0, -1):
            @pl.when(target > g)
            def _():
                ready_copy(g, target, p).start()

    def solve(p, count):
        these = pl.ds(pl.multiple_of(p * size, size), count * size)
        result[these] = ready[these]
        for h in range(groups - 1):
            @pl.when(h < g)
            def _():
                for i in range(count):
                    ready_copy(h, 0, p + i).wait_recv()
                result[these] = result[these] - apply_right(got[h, these], mix_t.at[h])

        @pl.when((p + count) % per == 0)
        def _():
            columns = pl.ds(pl.multiple_of((p // per) * LANES, LANES), LANES)
            out_ref[:, columns] = result[columns, :].T

    leads = [r + 1 if r else 0 for r in range(chips - 1)]
    order = [
        (r, q - leads[r]) for q in range(pieces + leads[-1]) for r in range(chips - 1)
        if 0 <= q - leads[r] < pieces]
    factor_load.wait()
    users_load(0, 0).wait()
    factor3[...] = left_form(factor[...])
    give[chip_at(0)] = dot(factor3[...], right_form(users[0])).T
    pl.semaphore_wait(
        barrier, groups + jnp.where(z > 0, 1, 0) + jnp.where(z < last, 1, 0))
    give_all(chip_at(0))
    product(0, 1)
    sender = jnp.logical_and(g > 0, g < groups - 1)
    edge = jnp.logical_or(z == 0, z == last)
    for j in range(chips):
        open_now = []
        while order and order[0][0] <= j:
            open_now.append(order.pop(0))
        if j == 0:
            pair_up(chip_at(0), open_now)
            product(1, 0)
            give_all(chip_at(1))
            for copy in later:
                copy.wait()

            @pl.when(jnp.logical_and(sender, jnp.logical_not(edge)))
            def _():
                prepare()

            product(1, 1)
        else:
            if j + 1 < chips:
                product(j + 1, 0)
                give_all(chip_at(j + 1))
            pair_up(chip_at(j), [])
            for r, p in open_now:
                launch(r, p)
            if j == 1:
                @pl.when(jnp.logical_and(sender, edge))
                def _():
                    prepare()

            if j + 1 < chips:
                product(j + 1, 1)

    behind = jnp.where(edge, chips // 2, leads[-1])

    @pl.loop(0, pieces + leads[-1] + WAIT)
    def _(q):
        @pl.when(q == 0)
        def _():
            turn()

        relay_near(q)

        @pl.when(jnp.logical_and(q == 1, g == groups - 1))
        def _():
            diag3[...] = left_form(diag[...])

        for h in range(groups - 1):
            @pl.when(jnp.logical_and(q == h + 1, g == groups - 1))
            def _():
                couple(h)

        p = q - behind

        @pl.when(jnp.logical_and(p >= 0, p < pieces))
        def _():
            finish(p)

        relay_far(q - LAG)

        pass_mix(q - PASS)

        join_mix(q - JOIN)
        p = q - behind - WAIT

        @pl.when(q == START)
        def _():
            solve(0, per)

        @pl.when(q >= START)
        def _():
            @pl.loop(jnp.where(q == START, per, jnp.maximum(p, per)), jnp.minimum(p + 1, pieces))
            def _(i):
                solve(i, 1)

    @pl.loop(0, chips)
    def _(d):
        @pl.when(d != z)
        def _():
            for p in range(pieces):
                pltpu.make_async_remote_copy(
                    src_ref=own.at[d, span(p)], dst_ref=from_low.at[d, span(p)],
                    send_sem=hop_sem.at[d, p], recv_sem=low_sem.at[d, p],
                    device_id=partner, device_id_type=MESH).wait_send()

    for target in range(1, groups):
        @pl.when(target > g)
        def _():
            for p in range(pieces):
                ready_copy(g, target, p).wait_send()
    for k, h in pairs:
        for target in range(k + 1, groups):
            @pl.when(g == k)
            def _():
                mix_copy(k, h, target).wait_send()


def by_kernel(right_side, solved_factor, solved_users, diag_inverse, coupling):
    groups = lax.axis_size("grp")
    chips = lax.axis_size("col") // 2
    rows, width = right_side.shape
    depth = solved_factor.shape[1]
    pieces = width // PIECE
    pairs = [(k, h) for k in range(1, groups - 1) for h in range(k)]
    f32, bf16 = jnp.float32, jnp.bfloat16
    dma = pltpu.SemaphoreType.DMA
    lines = pltpu.VMEM((chips, width, rows), f32)
    square = (rows, rows)
    scratch = [
        pltpu.VMEM((rows, width), f32),
        pltpu.VMEM((rows, depth), f32),
        pltpu.VMEM((2 * chips, depth, width), f32),
        pltpu.VMEM(square, f32),
        pltpu.VMEM(coupling.shape, f32),
        pltpu.VMEM((rows, 3 * depth), bf16),
        pltpu.VMEM((rows, 3 * rows), bf16),
        pltpu.VMEM((width, rows), f32),
        pltpu.VMEM((2,) + square, bf16),
        pltpu.VMEM((groups - 1, 2) + square, bf16),
        pltpu.VMEM((groups - 1,) + square, f32),
        pltpu.VMEM((groups - 1,) + square, f32),
        pltpu.VMEM((max(len(pairs), 1),) + square, f32),
        lines, lines, lines, lines, lines,
        pltpu.VMEM((width, rows), f32),
        pltpu.VMEM((groups - 1, width, rows), f32),
        pltpu.VMEM((width, rows), f32),
        dma((4,)), dma((2 * chips,)), dma((chips, pieces)), dma((chips, pieces)),
        dma((chips, pieces)), dma((chips, pieces)), dma((chips, pieces)),
        dma((groups, pieces)), dma((groups, pieces)),
        dma((max(len(pairs), 1), groups)), dma((max(len(pairs), 1),)),
        dma((max(len(pairs), 1),)), dma((max(len(pairs), 1),)),
    ]
    return pl.pallas_call(
        functools.partial(kernel, groups, chips, pieces, pairs),
        out_shape=pltpu.VMEM((rows, width), f32),
        in_specs=[pl.BlockSpec(memory_space=pl.ANY)] * 5,
        out_specs=pl.BlockSpec(memory_space=pltpu.VMEM),
        scratch_shapes=scratch,
        compiler_params=pltpu.CompilerParams(
            collective_id=0, has_side_effects=True, vmem_limit_bytes=63 << 20),
    )(right_side, solved_factor, solved_users, diag_inverse, coupling)


def on_device(right_side, *others):
    whole_tiles = (
        right_side.shape[1] % LANES == 0 and right_side.shape[0] % LANES == 0
        and lax.axis_size("col") % 2 == 0 and lax.axis_size("col") > 4
        and lax.axis_size("grp") > 1)
    return (by_kernel if whole_tiles else by_collectives)(right_side, *others)


def solution(mesh):
    placed = (P("grp", "col"), P("grp", "col"), P("col", None), P("grp", None), P("grp", None))
    return jax.shard_map(
        on_device, mesh=mesh, in_specs=placed, out_specs=P("grp", "col"), check_vma=False
    )
```

```python
import functools

import jax
import jax.numpy as jnp
from jax import lax
from jax.experimental import pallas as pl
from jax.experimental.pallas import tpu as pltpu
from jax.sharding import PartitionSpec as P

highest = lax.Precision.HIGHEST
MESH = pl.DeviceIdType.MESH
LANES = 128
PIECE = 32
LAG = 1
WAIT = 1
PASS = 5
JOIN = 6
START = 7
EDGE_PASS = 5
EDGE_JOIN = 6
EDGE_START = 7


def broadcast(block, axis, source):
    block = jnp.where(lax.axis_index(axis) == source, block, jnp.zeros_like(block))
    return lax.psum(block, axis)


def apply_plain(matrix, vector):
    return jnp.dot(matrix, vector, precision=highest, preferred_element_type=jnp.float32)


def run_chain(residue, diag_inverse, coupling, apply_left):
    groups = lax.axis_size("grp")
    position = lax.axis_index("grp")
    block_rows = diag_inverse.shape[0]
    result = jnp.zeros_like(residue)
    for section_index in range(groups):
        candidate = apply_left(diag_inverse, residue)
        result = jnp.where(position == section_index, candidate, result)
        if section_index + 1 < groups:
            solved = broadcast(candidate, "grp", section_index)
            coupling_block = coupling[
                :, section_index * block_rows : (section_index + 1) * block_rows
            ]
            residue = jnp.where(
                position > section_index, residue - apply_left(coupling_block, solved), residue
            )
    return result


def by_collectives(right_side, solved_factor, solved_users, diag_inverse, coupling):
    partials = jnp.dot(
        solved_factor, solved_users, precision=highest, preferred_element_type=jnp.float32
    )
    shares = lax.psum_scatter(partials, "col", scatter_dimension=1, tiled=True)
    residue = right_side - shares
    return run_chain(residue, diag_inverse, coupling, apply_plain)


def halves(x):
    high = x.astype(jnp.bfloat16)
    return high, (x - high.astype(jnp.float32)).astype(jnp.bfloat16)


def left_form(x):
    high, low = halves(x)
    return jnp.concatenate([high, high, low], axis=1)


def right_form(x):
    high, low = halves(x)
    return jnp.concatenate([high, low, high], axis=0)


def dot(a, b):
    return jnp.dot(a, b, preferred_element_type=jnp.float32)


def apply_right(rows, matrix):
    count = rows.shape[0]
    high, low = halves(rows)
    both = dot(jnp.concatenate([high, low], axis=0), matrix[0])
    return both[:count] + both[count:] + dot(high, matrix[1])


def kernel(
    groups, chips, pieces, pairs,
    rhs_hbm, factor_hbm, users_hbm, diag_hbm, coupling_hbm,
    out_ref,
    rhs, factor, users, diag, coupling,
    factor3, diag3, rhs_t, diag_t, mix_t, mix, blend, mix_in,
    own, give, take, from_low, from_high, ready, got, result,
    load_sem, users_sem, give_sem, take_sem, hop_sem, low_sem, high_sem,
    ready_sem, got_sem, mix_send_sem, mix_sem, pass_sem, passed_sem,
):
    g = lax.axis_index("grp")
    c = lax.axis_index("col")
    z = c // 2
    e = c % 2
    rows, width = rhs.shape
    half = rows // 2
    size = width // pieces
    last = chips - 1
    per = LANES // size
    partner = (g, z * 2 + (1 - e))
    lower = 2 * z < chips

    barrier = pltpu.get_barrier_semaphore()
    pl.semaphore_signal(barrier, inc=1, device_id=partner, device_id_type=MESH)
    for step in range(1, groups):
        pl.semaphore_signal(
            barrier, inc=1, device_id=((g + step) % groups, c), device_id_type=MESH)

    @pl.when(z > 0)
    def _():
        pl.semaphore_signal(barrier, inc=1, device_id=(g, c - 2), device_id_type=MESH)

    @pl.when(z < last)
    def _():
        pl.semaphore_signal(barrier, inc=1, device_id=(g, c + 2), device_id_type=MESH)

    def chip_at(j):
        if j == last:
            return z
        high, low = last - j, j
        return jnp.where(
            lower, jnp.where(high <= z, high - 1, high), jnp.where(low >= z, low + 1, low))

    factor_load = pltpu.make_async_copy(factor_hbm, factor, load_sem.at[0])
    later = [
        pltpu.make_async_copy(diag_hbm, diag, load_sem.at[1]),
        pltpu.make_async_copy(coupling_hbm, coupling, load_sem.at[2]),
        pltpu.make_async_copy(rhs_hbm, rhs, load_sem.at[3]),
    ]

    def users_load(j, part):
        side = e if part else 1 - e
        column = pl.multiple_of((chip_at(j) * 2 + side) * width, width)
        return pltpu.make_async_copy(
            users_hbm.at[:, pl.ds(column, width)], users.at[2 * j + part],
            users_sem.at[2 * j + part])

    factor_load.start()
    for part in range(2):
        users_load(0, part).start()

    def span(p):
        return pl.ds(pl.multiple_of(p * size, size), size)

    def give_copy(d, p):
        return pltpu.make_async_remote_copy(
            src_ref=give.at[d, span(p)], dst_ref=take.at[d, span(p)],
            send_sem=give_sem.at[d, p], recv_sem=take_sem.at[d, p],
            device_id=partner, device_id_type=MESH)

    def up(d, p):
        return pltpu.make_async_remote_copy(
            src_ref=own.at[d, span(p)], dst_ref=from_low.at[d, span(p)],
            send_sem=hop_sem.at[d, p], recv_sem=low_sem.at[d, p],
            device_id=(g, c + 2), device_id_type=MESH)

    def down(d, p):
        return pltpu.make_async_remote_copy(
            src_ref=own.at[d, span(p)], dst_ref=from_high.at[d, span(p)],
            send_sem=hop_sem.at[d, p], recv_sem=high_sem.at[d, p],
            device_id=(g, c - 2), device_id_type=MESH)

    def product(j, part):
        users_load(j, part).wait()
        block = dot(factor3[...], right_form(users[2 * j + part])).T
        (own if part else give)[chip_at(j)] = block

    def pair_up(d, at_once):
        @pl.loop(0, pieces)
        def _(p):
            give_copy(d, p).wait()
            own[d, span(p)] = own[d, span(p)] + take[d, span(p)]
            for r, i in at_once:
                @pl.when(p == i)
                def _():
                    launch(r, i)

    def launch(r, p):
        @pl.when(z == 0)
        def _():
            up(last - r, p).start()

        @pl.when(z == last)
        def _():
            down(r, p).start()

    def give_all(d):
        @pl.loop(0, pieces)
        def _(p):
            give_copy(d, p).start()

    def relay_up(r, p):
        d = last - r

        @pl.when(jnp.logical_and(z > 0, d > z))
        def _():
            up(d, p).wait_recv()
            own[d, span(p)] = own[d, span(p)] + from_low[d, span(p)]
            up(d, p).start()

    def relay_down(d, p):
        @pl.when(jnp.logical_and(z < last, d < z))
        def _():
            down(d, p).wait_recv()
            own[d, span(p)] = own[d, span(p)] + from_high[d, span(p)]
            down(d, p).start()

    def relay_near(q):
        for r in range(chips - 2):
            p = q - leads[r]

            @pl.when(jnp.logical_and(p >= 0, p < pieces))
            def _():
                @pl.when(lower)
                def _():
                    relay_up(r, p)

                @pl.when(jnp.logical_not(lower))
                def _():
                    relay_down(r, p)

    def relay_far(q):
        for r in range(chips // 2 - 1):
            p = q - leads[r]

            @pl.when(jnp.logical_and(p >= 0, p < pieces))
            def _():
                @pl.when(lower)
                def _():
                    relay_down(r, p)

                @pl.when(jnp.logical_not(lower))
                def _():
                    relay_up(r, p)

    def mix_copy(k, h, target):
        part = pl.ds(pl.multiple_of(e * half, half), half)
        i = pairs.index((k, h))
        return pltpu.make_async_remote_copy(
            src_ref=mix.at[h, part], dst_ref=mix_in.at[i, part],
            send_sem=mix_send_sem.at[i, target], recv_sem=mix_sem.at[i],
            device_id=(target, c), device_id_type=MESH)

    def mix_pass(k, h):
        part = pl.ds(pl.multiple_of(e * half, half), half)
        i = pairs.index((k, h))
        return pltpu.make_async_remote_copy(
            src_ref=mix_in.at[i, part], dst_ref=mix_in.at[i, part],
            send_sem=pass_sem.at[i], recv_sem=passed_sem.at[i],
            device_id=partner, device_id_type=MESH)

    def couple(h):
        effect = dot(diag3[...], right_form(coupling[:, h * rows : (h + 1) * rows]))
        mix[h] = effect
        blend[h] = effect

        @pl.when(g == h + 1)
        def _():
            high, low = halves(effect.T)
            mix_t[h, 0] = high
            mix_t[h, 1] = low

    def prepare():
        diag3[...] = left_form(diag[...])
        for h in range(groups - 2):
            @pl.when(h < g)
            def _():
                couple(h)
        for k, h in pairs:
            for target in range(k + 1, groups):
                @pl.when(g == k)
                def _():
                    mix_copy(k, h, target).start()

    def turn():
        rhs_t[...] = rhs[...].T
        high, low = halves(diag[...].T)
        diag_t[0] = high
        diag_t[1] = low

    def pass_mix(step):
        for k, h in pairs:
            @pl.when(jnp.logical_and(g > k, step == k - 1))
            def _():
                mix_copy(k, h, k + 1).wait_recv()
                mix_pass(k, h).start()

    def join_mix(step):
        for n, k in enumerate(range(groups - 2, 0, -1)):
            @pl.when(jnp.logical_and(g > k, step == n))
            def _():
                for h in range(k):
                    mix_pass(k, h).wait()
                left = left_form(blend[k])
                for h in range(k):
                    right = right_form(mix_in[pairs.index((k, h))])
                    blend[h] = blend[h] - dot(left, right)

        @pl.when(step == max(groups - 3, 0))
        def _():
            for h in range(groups - 2):
                @pl.when(h < g - 1)
                def _():
                    high, low = halves(blend[h].T)
                    mix_t[h, 0] = high
                    mix_t[h, 1] = low

    def ready_copy(source, target, p):
        return pltpu.make_async_remote_copy(
            src_ref=ready.at[span(p)], dst_ref=got.at[source, span(p)],
            send_sem=ready_sem.at[target, p], recv_sem=got_sem.at[source, p],
            device_id=(target, c), device_id_type=MESH)

    def finish(p):
        @pl.when(z > 0)
        def _():
            up(z, p).wait_recv()
            own[z, span(p)] = own[z, span(p)] + from_low[z, span(p)]

        @pl.when(z < last)
        def _():
            down(z, p).wait_recv()
            own[z, span(p)] = own[z, span(p)] + from_high[z, span(p)]

        ready[span(p)] = apply_right(rhs_t[span(p)] - own[z, span(p)], diag_t)

        for target in range(groups - 1, 0, -1):
            @pl.when(target > g)
            def _():
                ready_copy(g, target, p).start()

    def solve(p, count):
        these = pl.ds(pl.multiple_of(p * size, size), count * size)
        result[these] = ready[these]
        for h in range(groups - 1):
            @pl.when(h < g)
            def _():
                for i in range(count):
                    ready_copy(h, 0, p + i).wait_recv()
                result[these] = result[these] - apply_right(got[h, these], mix_t.at[h])

        @pl.when((p + count) % per == 0)
        def _():
            columns = pl.ds(pl.multiple_of((p // per) * LANES, LANES), LANES)
            out_ref[:, columns] = result[columns, :].T

    leads = [r + 1 if r else 0 for r in range(chips - 1)]
    order = [
        (r, q - leads[r]) for q in range(pieces + leads[-1]) for r in range(chips - 1)
        if 0 <= q - leads[r] < pieces]
    factor_load.wait()
    users_load(0, 0).wait()
    for j in range(1, chips):
        for part in range(2):
            users_load(j, part).start()
    for copy in later:
        copy.start()
    factor3[...] = left_form(factor[...])
    give[chip_at(0)] = dot(factor3[...], right_form(users[0])).T
    pl.semaphore_wait(
        barrier, groups + jnp.where(z > 0, 1, 0) + jnp.where(z < last, 1, 0))
    give_all(chip_at(0))
    product(0, 1)
    sender = jnp.logical_and(g > 0, g < groups - 1)
    edge = jnp.logical_or(z == 0, z == last)
    for j in range(chips):
        open_now = []
        while order and order[0][0] <= j:
            open_now.append(order.pop(0))
        if j == 0:
            pair_up(chip_at(0), open_now)
            product(1, 0)
            give_all(chip_at(1))
            for copy in later:
                copy.wait()

            @pl.when(jnp.logical_and(sender, jnp.logical_not(edge)))
            def _():
                prepare()

            product(1, 1)
        else:
            if j + 1 < chips:
                product(j + 1, 0)
                give_all(chip_at(j + 1))
            pair_up(chip_at(j), [])
            for r, p in open_now:
                launch(r, p)
            if j == 1:
                @pl.when(jnp.logical_and(sender, edge))
                def _():
                    prepare()

            if j + 1 < chips:
                product(j + 1, 1)

    behind = jnp.where(edge, chips // 2, leads[-1])
    passing = jnp.where(edge, EDGE_PASS, PASS)
    joining = jnp.where(edge, EDGE_JOIN, JOIN)
    starting = jnp.where(edge, EDGE_START, START)

    @pl.loop(0, pieces + leads[-1] + WAIT)
    def _(q):
        @pl.when(q == 0)
        def _():
            turn()

        relay_near(q)

        @pl.when(jnp.logical_and(q == 1, g == groups - 1))
        def _():
            diag3[...] = left_form(diag[...])

        for h in range(groups - 1):
            @pl.when(jnp.logical_and(q == h + 1, g == groups - 1))
            def _():
                couple(h)

        p = q - behind

        @pl.when(jnp.logical_and(p >= 0, p < pieces))
        def _():
            finish(p)

        relay_far(q - LAG)

        pass_mix(q - passing)

        join_mix(q - joining)
        p = q - behind - WAIT

        @pl.when(q == starting)
        def _():
            solve(0, per)

        @pl.when(q >= starting)
        def _():
            @pl.loop(jnp.where(q == starting, per, jnp.maximum(p, per)), jnp.minimum(p + 1, pieces))
            def _(i):
                solve(i, 1)

    @pl.loop(0, chips)
    def _(d):
        @pl.when(d != z)
        def _():
            for p in range(pieces):
                pltpu.make_async_remote_copy(
                    src_ref=own.at[d, span(p)], dst_ref=from_low.at[d, span(p)],
                    send_sem=hop_sem.at[d, p], recv_sem=low_sem.at[d, p],
                    device_id=partner, device_id_type=MESH).wait_send()

    for target in range(1, groups):
        @pl.when(target > g)
        def _():
            for p in range(pieces):
                ready_copy(g, target, p).wait_send()
    for k, h in pairs:
        for target in range(k + 1, groups):
            @pl.when(g == k)
            def _():
                mix_copy(k, h, target).wait_send()


def by_kernel(right_side, solved_factor, solved_users, diag_inverse, coupling):
    groups = lax.axis_size("grp")
    chips = lax.axis_size("col") // 2
    rows, width = right_side.shape
    depth = solved_factor.shape[1]
    pieces = width // PIECE
    pairs = [(k, h) for k in range(1, groups - 1) for h in range(k)]
    f32, bf16 = jnp.float32, jnp.bfloat16
    dma = pltpu.SemaphoreType.DMA
    lines = pltpu.VMEM((chips, width, rows), f32)
    square = (rows, rows)
    scratch = [
        pltpu.VMEM((rows, width), f32),
        pltpu.VMEM((rows, depth), f32),
        pltpu.VMEM((2 * chips, depth, width), f32),
        pltpu.VMEM(square, f32),
        pltpu.VMEM(coupling.shape, f32),
        pltpu.VMEM((rows, 3 * depth), bf16),
        pltpu.VMEM((rows, 3 * rows), bf16),
        pltpu.VMEM((width, rows), f32),
        pltpu.VMEM((2,) + square, bf16),
        pltpu.VMEM((groups - 1, 2) + square, bf16),
        pltpu.VMEM((groups - 1,) + square, f32),
        pltpu.VMEM((groups - 1,) + square, f32),
        pltpu.VMEM((max(len(pairs), 1),) + square, f32),
        lines, lines, lines, lines, lines,
        pltpu.VMEM((width, rows), f32),
        pltpu.VMEM((groups - 1, width, rows), f32),
        pltpu.VMEM((width, rows), f32),
        dma((4,)), dma((2 * chips,)), dma((chips, pieces)), dma((chips, pieces)),
        dma((chips, pieces)), dma((chips, pieces)), dma((chips, pieces)),
        dma((groups, pieces)), dma((groups, pieces)),
        dma((max(len(pairs), 1), groups)), dma((max(len(pairs), 1),)),
        dma((max(len(pairs), 1),)), dma((max(len(pairs), 1),)),
    ]
    return pl.pallas_call(
        functools.partial(kernel, groups, chips, pieces, pairs),
        out_shape=pltpu.VMEM((rows, width), f32),
        in_specs=[pl.BlockSpec(memory_space=pl.ANY)] * 5,
        out_specs=pl.BlockSpec(memory_space=pltpu.VMEM),
        scratch_shapes=scratch,
        compiler_params=pltpu.CompilerParams(
            collective_id=0, has_side_effects=True, vmem_limit_bytes=63 << 20),
    )(right_side, solved_factor, solved_users, diag_inverse, coupling)


def on_device(right_side, *others):
    whole_tiles = (
        right_side.shape[1] % LANES == 0 and right_side.shape[0] % LANES == 0
        and lax.axis_size("col") % 2 == 0 and lax.axis_size("col") > 4
        and lax.axis_size("grp") > 1)
    return (by_kernel if whole_tiles else by_collectives)(right_side, *others)


def solution(mesh):
    placed = (P("grp", "col"), P("grp", "col"), P("col", None), P("grp", None), P("grp", None))
    return jax.shard_map(
        on_device, mesh=mesh, in_specs=placed, out_specs=P("grp", "col"), check_vma=False
    )
```

```python
import functools

import jax
import jax.numpy as jnp
from jax import lax
from jax.experimental import pallas as pl
from jax.experimental.pallas import tpu as pltpu
from jax.sharding import PartitionSpec as P

highest = lax.Precision.HIGHEST
MESH = pl.DeviceIdType.MESH
LANES = 128
PIECE = 32
LAG = 1
WAIT = 1
PASS = 5
JOIN = 6
START = 7
EDGE_PASS = 5
EDGE_JOIN = 6
EDGE_START = 7


def broadcast(block, axis, source):
    block = jnp.where(lax.axis_index(axis) == source, block, jnp.zeros_like(block))
    return lax.psum(block, axis)


def apply_plain(matrix, vector):
    return jnp.dot(matrix, vector, precision=highest, preferred_element_type=jnp.float32)


def run_chain(residue, diag_inverse, coupling, apply_left):
    groups = lax.axis_size("grp")
    position = lax.axis_index("grp")
    block_rows = diag_inverse.shape[0]
    result = jnp.zeros_like(residue)
    for section_index in range(groups):
        candidate = apply_left(diag_inverse, residue)
        result = jnp.where(position == section_index, candidate, result)
        if section_index + 1 < groups:
            solved = broadcast(candidate, "grp", section_index)
            coupling_block = coupling[
                :, section_index * block_rows : (section_index + 1) * block_rows
            ]
            residue = jnp.where(
                position > section_index, residue - apply_left(coupling_block, solved), residue
            )
    return result


def by_collectives(right_side, solved_factor, solved_users, diag_inverse, coupling):
    partials = jnp.dot(
        solved_factor, solved_users, precision=highest, preferred_element_type=jnp.float32
    )
    shares = lax.psum_scatter(partials, "col", scatter_dimension=1, tiled=True)
    residue = right_side - shares
    return run_chain(residue, diag_inverse, coupling, apply_plain)


def halves(x):
    high = x.astype(jnp.bfloat16)
    return high, (x - high.astype(jnp.float32)).astype(jnp.bfloat16)


def left_form(x):
    high, low = halves(x)
    return jnp.concatenate([high, high, low], axis=1)


def right_form(x):
    high, low = halves(x)
    return jnp.concatenate([high, low, high], axis=0)


def dot(a, b):
    return jnp.dot(a, b, preferred_element_type=jnp.float32)


def apply_right(rows, matrix):
    count = rows.shape[0]
    high, low = halves(rows)
    both = dot(jnp.concatenate([high, low], axis=0), matrix[0])
    return both[:count] + both[count:] + dot(high, matrix[1])


def kernel(
    groups, chips, pieces, pairs,
    rhs_hbm, factor_hbm, users_hbm, diag_hbm, coupling_hbm,
    out_ref,
    rhs, factor, users, diag, coupling,
    factor3, diag3, rhs_t, diag_t, mix_t, mix, blend, mix_in,
    own, give, take, from_low, from_high, ready, got, result,
    load_sem, users_sem, give_sem, take_sem, hop_sem, low_sem, high_sem,
    ready_sem, got_sem, mix_send_sem, mix_sem, pass_sem, passed_sem,
):
    g = lax.axis_index("grp")
    c = lax.axis_index("col")
    z = c // 2
    e = c % 2
    rows, width = rhs.shape
    half = rows // 2
    size = width // pieces
    last = chips - 1
    per = LANES // size
    partner = (g, z * 2 + (1 - e))
    lower = 2 * z < chips

    barrier = pltpu.get_barrier_semaphore()
    pl.semaphore_signal(barrier, inc=1, device_id=partner, device_id_type=MESH)
    for step in range(1, groups):
        pl.semaphore_signal(
            barrier, inc=1, device_id=((g + step) % groups, c), device_id_type=MESH)

    @pl.when(z > 0)
    def _():
        pl.semaphore_signal(barrier, inc=1, device_id=(g, c - 2), device_id_type=MESH)

    @pl.when(z < last)
    def _():
        pl.semaphore_signal(barrier, inc=1, device_id=(g, c + 2), device_id_type=MESH)

    def chip_at(j):
        if j == last:
            return z
        high, low = last - j, j
        return jnp.where(
            lower, jnp.where(high <= z, high - 1, high), jnp.where(low >= z, low + 1, low))

    factor_load = pltpu.make_async_copy(factor_hbm, factor, load_sem.at[0])
    later = [
        pltpu.make_async_copy(diag_hbm, diag, load_sem.at[1]),
        pltpu.make_async_copy(coupling_hbm, coupling, load_sem.at[2]),
        pltpu.make_async_copy(rhs_hbm, rhs, load_sem.at[3]),
    ]

    def users_load(j, part):
        side = e if part else 1 - e
        column = pl.multiple_of((chip_at(j) * 2 + side) * width, width)
        return pltpu.make_async_copy(
            users_hbm.at[:, pl.ds(column, width)], users.at[2 * j + part],
            users_sem.at[2 * j + part])

    factor_load.start()
    for part in range(2):
        users_load(0, part).start()

    def span(p):
        return pl.ds(pl.multiple_of(p * size, size), size)

    def give_copy(d, p):
        return pltpu.make_async_remote_copy(
            src_ref=give.at[d, span(p)], dst_ref=take.at[d, span(p)],
            send_sem=give_sem.at[d, p], recv_sem=take_sem.at[d, p],
            device_id=partner, device_id_type=MESH)

    def up(d, p):
        return pltpu.make_async_remote_copy(
            src_ref=own.at[d, span(p)], dst_ref=from_low.at[d, span(p)],
            send_sem=hop_sem.at[d, p], recv_sem=low_sem.at[d, p],
            device_id=(g, c + 2), device_id_type=MESH)

    def down(d, p):
        return pltpu.make_async_remote_copy(
            src_ref=own.at[d, span(p)], dst_ref=from_high.at[d, span(p)],
            send_sem=hop_sem.at[d, p], recv_sem=high_sem.at[d, p],
            device_id=(g, c - 2), device_id_type=MESH)

    def product(j, part):
        users_load(j, part).wait()
        block = dot(factor3[...], right_form(users[2 * j + part])).T
        (own if part else give)[chip_at(j)] = block

    def pair_up(d, at_once):
        @pl.loop(0, pieces)
        def _(p):
            give_copy(d, p).wait()
            own[d, span(p)] = own[d, span(p)] + take[d, span(p)]
            for r, i in at_once:
                @pl.when(p == i)
                def _():
                    launch(r, i)

    def launch(r, p):
        @pl.when(z == 0)
        def _():
            up(last - r, p).start()

        @pl.when(z == last)
        def _():
            down(r, p).start()

    def give_all(d):
        @pl.loop(0, pieces)
        def _(p):
            give_copy(d, p).start()

    def relay_up(r, p):
        d = last - r

        @pl.when(jnp.logical_and(z > 0, d > z))
        def _():
            up(d, p).wait_recv()
            own[d, span(p)] = own[d, span(p)] + from_low[d, span(p)]
            up(d, p).start()

    def relay_down(d, p):
        @pl.when(jnp.logical_and(z < last, d < z))
        def _():
            down(d, p).wait_recv()
            own[d, span(p)] = own[d, span(p)] + from_high[d, span(p)]
            down(d, p).start()

    def relay_near(q):
        for r in range(chips - 2):
            p = q - leads[r]

            @pl.when(jnp.logical_and(p >= 0, p < pieces))
            def _():
                @pl.when(lower)
                def _():
                    relay_up(r, p)

                @pl.when(jnp.logical_not(lower))
                def _():
                    relay_down(r, p)

    def relay_far(q):
        for r in range(chips // 2 - 1):
            p = q - leads[r]

            @pl.when(jnp.logical_and(p >= 0, p < pieces))
            def _():
                @pl.when(lower)
                def _():
                    relay_down(r, p)

                @pl.when(jnp.logical_not(lower))
                def _():
                    relay_up(r, p)

    def mix_copy(k, h, target):
        part = pl.ds(pl.multiple_of(e * half, half), half)
        i = pairs.index((k, h))
        return pltpu.make_async_remote_copy(
            src_ref=mix.at[h, part], dst_ref=mix_in.at[i, part],
            send_sem=mix_send_sem.at[i, target], recv_sem=mix_sem.at[i],
            device_id=(target, c), device_id_type=MESH)

    def mix_pass(k, h):
        part = pl.ds(pl.multiple_of(e * half, half), half)
        i = pairs.index((k, h))
        return pltpu.make_async_remote_copy(
            src_ref=mix_in.at[i, part], dst_ref=mix_in.at[i, part],
            send_sem=pass_sem.at[i], recv_sem=passed_sem.at[i],
            device_id=partner, device_id_type=MESH)

    def couple(h):
        effect = dot(diag3[...], right_form(coupling[:, h * rows : (h + 1) * rows]))
        mix[h] = effect
        blend[h] = effect

        @pl.when(g == h + 1)
        def _():
            high, low = halves(effect.T)
            mix_t[h, 0] = high
            mix_t[h, 1] = low

    def prepare():
        diag3[...] = left_form(diag[...])
        for h in range(groups - 2):
            @pl.when(h < g)
            def _():
                couple(h)
            for k in range(h + 1, groups - 1):
                for target in range(k + 1, groups):
                    @pl.when(g == k)
                    def _():
                        mix_copy(k, h, target).start()

    def turn():
        rhs_t[...] = rhs[...].T
        high, low = halves(diag[...].T)
        diag_t[0] = high
        diag_t[1] = low

    def pass_mix(step):
        for k, h in pairs:
            @pl.when(jnp.logical_and(g > k, step == k - 1))
            def _():
                mix_copy(k, h, k + 1).wait_recv()
                mix_pass(k, h).start()

    def join_mix(step):
        for n, k in enumerate(range(groups - 2, 0, -1)):
            @pl.when(jnp.logical_and(g > k, step == n))
            def _():
                for h in range(k):
                    mix_pass(k, h).wait()
                left = left_form(blend[k])
                for h in range(k):
                    right = right_form(mix_in[pairs.index((k, h))])
                    blend[h] = blend[h] - dot(left, right)

        @pl.when(step == max(groups - 3, 0))
        def _():
            for h in range(groups - 2):
                @pl.when(h < g - 1)
                def _():
                    high, low = halves(blend[h].T)
                    mix_t[h, 0] = high
                    mix_t[h, 1] = low

    def ready_copy(source, target, p):
        return pltpu.make_async_remote_copy(
            src_ref=ready.at[span(p)], dst_ref=got.at[source, span(p)],
            send_sem=ready_sem.at[target, p], recv_sem=got_sem.at[source, p],
            device_id=(target, c), device_id_type=MESH)

    def finish(p):
        @pl.when(z > 0)
        def _():
            up(z, p).wait_recv()
            own[z, span(p)] = own[z, span(p)] + from_low[z, span(p)]

        @pl.when(z < last)
        def _():
            down(z, p).wait_recv()
            own[z, span(p)] = own[z, span(p)] + from_high[z, span(p)]

        ready[span(p)] = apply_right(rhs_t[span(p)] - own[z, span(p)], diag_t)

        for target in range(groups - 1, 0, -1):
            @pl.when(target > g)
            def _():
                ready_copy(g, target, p).start()

    def solve(p, count):
        these = pl.ds(pl.multiple_of(p * size, size), count * size)
        result[these] = ready[these]

        def subtract(h):
            for i in range(count):
                ready_copy(h, 0, p + i).wait_recv()
            result[these] = result[these] - apply_right(got[h, these], mix_t.at[h])

        for h in range(groups - 2, 0, -1):
            @pl.when(g == groups - 1)
            def _():
                subtract(h)

        for h in range(groups - 1):
            @pl.when(jnp.logical_and(h < g, jnp.logical_or(h == 0, g < groups - 1)))
            def _():
                subtract(h)

        @pl.when((p + count) % per == 0)
        def _():
            columns = pl.ds(pl.multiple_of((p // per) * LANES, LANES), LANES)
            out_ref[:, columns] = result[columns, :].T

    leads = [r + 1 if r else 0 for r in range(chips - 1)]
    order = [
        (r, q - leads[r]) for q in range(pieces + leads[-1]) for r in range(chips - 1)
        if 0 <= q - leads[r] < pieces]
    factor_load.wait()
    users_load(0, 0).wait()
    for j in range(1, chips):
        for part in range(2):
            users_load(j, part).start()
    for copy in later:
        copy.start()
    factor3[...] = left_form(factor[...])
    give[chip_at(0)] = dot(factor3[...], right_form(users[0])).T
    pl.semaphore_wait(
        barrier, groups + jnp.where(z > 0, 1, 0) + jnp.where(z < last, 1, 0))
    give_all(chip_at(0))
    product(0, 1)
    sender = jnp.logical_and(g > 0, g < groups - 1)
    edge = jnp.logical_or(z == 0, z == last)
    for j in range(chips):
        open_now = []
        while order and order[0][0] <= j:
            open_now.append(order.pop(0))
        if j == 0:
            pair_up(chip_at(0), open_now)
            product(1, 0)
            give_all(chip_at(1))
            for copy in later:
                copy.wait()

            @pl.when(jnp.logical_and(sender, jnp.logical_not(edge)))
            def _():
                prepare()

            product(1, 1)
        else:
            if j + 1 < chips:
                product(j + 1, 0)
                give_all(chip_at(j + 1))
            pair_up(chip_at(j), [])
            for r, p in open_now:
                launch(r, p)
            if j == 1:
                @pl.when(jnp.logical_and(sender, edge))
                def _():
                    prepare()

            if j + 1 < chips:
                product(j + 1, 1)

    behind = jnp.where(edge, chips // 2, leads[-1])
    passing = jnp.where(edge, EDGE_PASS, PASS)
    joining = jnp.where(edge, EDGE_JOIN, JOIN)
    starting = jnp.where(edge, EDGE_START, START)

    @pl.loop(0, pieces + leads[-1] + WAIT)
    def _(q):
        @pl.when(q == 0)
        def _():
            turn()

        relay_near(q)

        @pl.when(jnp.logical_and(q == 1, g == groups - 1))
        def _():
            diag3[...] = left_form(diag[...])

        for h in range(groups - 1):
            @pl.when(jnp.logical_and(q == h + 1, g == groups - 1))
            def _():
                couple(h)

        pass_mix(q - passing)
        p = q - behind

        @pl.when(jnp.logical_and(p >= 0, p < pieces))
        def _():
            finish(p)

        relay_far(q - LAG)


        join_mix(q - joining)
        p = q - behind - WAIT

        @pl.when(q == starting)
        def _():
            solve(0, per)

        @pl.when(q >= starting)
        def _():
            @pl.loop(jnp.where(q == starting, per, jnp.maximum(p, per)), jnp.minimum(p + 1, pieces))
            def _(i):
                solve(i, 1)

    @pl.loop(0, chips)
    def _(d):
        @pl.when(d != z)
        def _():
            for p in range(pieces):
                pltpu.make_async_remote_copy(
                    src_ref=own.at[d, span(p)], dst_ref=from_low.at[d, span(p)],
                    send_sem=hop_sem.at[d, p], recv_sem=low_sem.at[d, p],
                    device_id=partner, device_id_type=MESH).wait_send()

    for target in range(1, groups):
        @pl.when(target > g)
        def _():
            for p in range(pieces):
                ready_copy(g, target, p).wait_send()
    for k, h in pairs:
        for target in range(k + 1, groups):
            @pl.when(g == k)
            def _():
                mix_copy(k, h, target).wait_send()


def by_kernel(right_side, solved_factor, solved_users, diag_inverse, coupling):
    groups = lax.axis_size("grp")
    chips = lax.axis_size("col") // 2
    rows, width = right_side.shape
    depth = solved_factor.shape[1]
    pieces = width // PIECE
    pairs = [(k, h) for k in range(1, groups - 1) for h in range(k)]
    f32, bf16 = jnp.float32, jnp.bfloat16
    dma = pltpu.SemaphoreType.DMA
    lines = pltpu.VMEM((chips, width, rows), f32)
    square = (rows, rows)
    scratch = [
        pltpu.VMEM((rows, width), f32),
        pltpu.VMEM((rows, depth), f32),
        pltpu.VMEM((2 * chips, depth, width), f32),
        pltpu.VMEM(square, f32),
        pltpu.VMEM(coupling.shape, f32),
        pltpu.VMEM((rows, 3 * depth), bf16),
        pltpu.VMEM((rows, 3 * rows), bf16),
        pltpu.VMEM((width, rows), f32),
        pltpu.VMEM((2,) + square, bf16),
        pltpu.VMEM((groups - 1, 2) + square, bf16),
        pltpu.VMEM((groups - 1,) + square, f32),
        pltpu.VMEM((groups - 1,) + square, f32),
        pltpu.VMEM((max(len(pairs), 1),) + square, f32),
        lines, lines, lines, lines, lines,
        pltpu.VMEM((width, rows), f32),
        pltpu.VMEM((groups - 1, width, rows), f32),
        pltpu.VMEM((width, rows), f32),
        dma((4,)), dma((2 * chips,)), dma((chips, pieces)), dma((chips, pieces)),
        dma((chips, pieces)), dma((chips, pieces)), dma((chips, pieces)),
        dma((groups, pieces)), dma((groups, pieces)),
        dma((max(len(pairs), 1), groups)), dma((max(len(pairs), 1),)),
        dma((max(len(pairs), 1),)), dma((max(len(pairs), 1),)),
    ]
    return pl.pallas_call(
        functools.partial(kernel, groups, chips, pieces, pairs),
        out_shape=pltpu.VMEM((rows, width), f32),
        in_specs=[pl.BlockSpec(memory_space=pl.ANY)] * 5,
        out_specs=pl.BlockSpec(memory_space=pltpu.VMEM),
        scratch_shapes=scratch,
        compiler_params=pltpu.CompilerParams(
            collective_id=0, has_side_effects=True, vmem_limit_bytes=63 << 20),
    )(right_side, solved_factor, solved_users, diag_inverse, coupling)


def on_device(right_side, *others):
    whole_tiles = (
        right_side.shape[1] % LANES == 0 and right_side.shape[0] % LANES == 0
        and lax.axis_size("col") % 2 == 0 and lax.axis_size("col") > 4
        and lax.axis_size("grp") > 1)
    return (by_kernel if whole_tiles else by_collectives)(right_side, *others)


def solution(mesh):
    placed = (P("grp", "col"), P("grp", "col"), P("col", None), P("grp", None), P("grp", None))
    return jax.shard_map(
        on_device, mesh=mesh, in_specs=placed, out_specs=P("grp", "col"), check_vma=False
    )
```
